32 devices in a mesh: seq: 8 (over z, y), geo: 4 (over x, core).
Axes of the slice: x: 2, y: 2, z: 4, core: 2. Of those that a mesh axis runs over, the one named last changes fastest.
Arguments:
- ssm_input: bfloat16 [8192, 768], P(('geo', 'seq')), parts along dimension 0, may hold values from -6 to 6
- gate_input: bfloat16 [8192, 768], P(('geo', 'seq')), parts along dimension 0, may hold values from -6 to 6
- state_proj: bfloat16 [8192, 128], P(('geo', 'seq')), parts along dimension 0, may hold values from -6 to 6
- step_raw: float32 [12, 8192], P(None, ('geo', 'seq')), parts along dimension 1, may hold values from -5 to 5
- decay_log: float32 [12], replicated, may hold values from -20 to 2
- step_bias: float32 [12], replicated, may hold values from -8 to -3
- skip_gain: float32 [12], replicated, may hold values from 0.5 to 1.5
- norm_gain: float32 [768], replicated, may hold values from 0.25 to 1.75
- out_weight: bfloat16 [768, 384], replicated, may hold values from -0.21875 to 0.21875
- block_counts: int32 [32, 8], P('geo'), parts along dimension 0, may hold values from 0 to 2, as said below
- out_cotangent: bfloat16 [8192, 384], P(('geo', 'seq')), parts along dimension 0, may hold values from -6 to 6
Outputs:
- mixed_points: bfloat16 [8192, 384], P(('geo', 'seq')), parts along dimension 0
- grad_input: bfloat16 [8192, 768], P(('geo', 'seq')), parts along dimension 0
- grad_gate: bfloat16 [8192, 768], P(('geo', 'seq')), parts along dimension 0
- grad_proj: bfloat16 [8192, 128], P(('geo', 'seq')), parts along dimension 0
- grad_step: float32 [12, 8192], P(None, ('geo', 'seq')), parts along dimension 1
- grad_weight: float32 [3072, 384], P('geo'), parts along dimension 0
- grad_heads: float32 [12, 12], P('geo'), parts along dimension 0
- grad_norm: float32 [3072], P('geo'), parts along dimension 0
The draws below stay inside these ranges and needn't reach their ends.
There are 4 independent parts, one for each index of `geo`. The reference program is written for one: setup_inputs(seed, part) draws one part's arguments, and reference() takes and returns one part's arrays. A program takes and returns all parts, laid end to end along the dimension named above; an argument that names none is the same for every part. Nothing has to cross between parts.
Inputs may be any that keep to these rules, and one draw needn't show every extreme that they name: block_counts[s, t] is the number of aligned blocks of 128 rows that shard s sends to shard t: symmetric, zero unless s and t differ by at most one, each row sums to 2; entries off the diagonal are at most 1, reached in every draw; shards 0 and 1 exchange exactly 1 block each way.
All inputs are finite; a program needn't handle non-finite values.
Results may differ from the reference program's by a relative error of at most 0.0049.
Values may be sent and summed in bfloat16 or wider, within the bound.
No kernel may reach another device: no remote copies, remote signals or barrier semaphores. Data moves between devices by JAX's collectives and lax.ppermute only.
A program may use at most 128 MiB of HBM per device.

```python
import jax
import jax.numpy as jnp
from jax import lax

D = 384
HEADS = 12
STATE = 64
ROWS_DEV = 256
BLOCK_ROWS = 128
GROUP = 256
DIN = 768
BLOCKS_DEV = 2
MOVE_MAX = 1
SHARDS = 8
POINTS = 2048


def head_rates(key):
    folded = jax.random.fold_in(key, 11)
    key_order, key_step, key_keep = jax.random.split(folded, 3)
    ranking = jax.random.permutation(key_order, HEADS)
    if HEADS >= 4:
        middle_quick = ranking == HEADS - 2
        middle_drawn = ranking == HEADS - 3
    else:
        middle_quick = ranking < 0
        middle_drawn = ranking < 0
    is_middle = middle_quick | middle_drawn
    is_slow = (ranking < (HEADS + 1) // 2) & ~is_middle
    fraction = jax.random.uniform(key_step, (HEADS,), jnp.float32)
    keeping = jax.random.uniform(key_keep, (HEADS,), jnp.float32)
    step_base = jnp.where(is_slow, 0.0005 * 4.0 ** fraction, 0.01 * 4.0 ** fraction)
    step_base = jnp.where(is_middle, 0.005 * 4.0 ** fraction, step_base)
    rate_slow = (0.3 + 1.2 * keeping) / (POINTS * 1.65 * step_base)
    rate_fast = 0.02 * 2.5 ** keeping / (1.65 * step_base)
    shard_loss = jnp.where(middle_quick, 0.5 + 0.5 * keeping, 0.2 + 0.15 * keeping)
    rate_middle = shard_loss / (ROWS_DEV * 1.65 * step_base)
    decay_rate = jnp.where(is_slow, rate_slow, rate_fast)
    decay_rate = jnp.where(is_middle, rate_middle, decay_rate)
    return (jnp.log(decay_rate), jnp.log(jnp.expm1(step_base)))


def draw_decay_log(key, part):
    return head_rates(key)[0]


def draw_step_bias(key, part):
    return head_rates(key)[1]


def draw_block_counts(key, part):
    folded = jax.random.fold_in(key, 23)
    key_moves, key_pick = jax.random.split(folded)
    shards = SHARDS
    move_counts = jax.random.randint(key_moves, (shards - 1,), 0, MOVE_MAX + 1, dtype=jnp.int32)
    chosen = jax.random.randint(key_pick, (), 1, shards - 1, dtype=jnp.int32)
    places = jnp.arange(shards - 1, dtype=jnp.int32)
    move_counts = jnp.where((places == 0) | (places == chosen), MOVE_MAX, move_counts)
    upward = jnp.concatenate([move_counts, jnp.zeros((1,), jnp.int32)])
    downward = jnp.concatenate([jnp.zeros((1,), jnp.int32), move_counts])
    row_ids = jnp.arange(shards, dtype=jnp.int32)[:, None]
    col_ids = jnp.arange(shards, dtype=jnp.int32)[None, :]
    counts = jnp.where(col_ids == row_ids + 1, upward[:, None], 0)
    counts = counts + jnp.where(col_ids == row_ids - 1, downward[:, None], 0)
    counts = counts + jnp.where(col_ids == row_ids, (BLOCKS_DEV - upward - downward)[:, None], 0)
    return counts.astype(jnp.int32)


def steps_of(stream_key, shape, cuts, low, high):
    factor_of, own = 1.0, jax.random.fold_in(stream_key, 6)
    for dim, blocks in cuts:
        heights = jnp.exp(jax.random.uniform(jax.random.fold_in(own, dim), (blocks,), jnp.float32, low / len(cuts), high / len(cuts)))
        factor_of = factor_of * jnp.repeat(heights, shape[dim] // blocks).reshape([-1 if axis == dim else 1 for axis in range(len(shape))])
    return factor_of


def noise(stream_key, shape, width, limit, cuts=(), held_as=jnp.bfloat16):
    entries = jax.random.normal(stream_key, shape, jnp.float32) * width
    if len(cuts) > 0:
        entries = steps_of(stream_key, shape, cuts, -0.22, 0.18) * entries
    return jnp.clip(entries, min=-limit, max=limit).astype(held_as)


def setup_inputs(seed: int = 0, part: int = 0) -> dict:
    streams_of = jax.random.split(jax.random.key(seed), 12)
    part_keys = jax.random.split(jax.random.fold_in(streams_of[11], part), 12)
    return {
        "ssm_input": noise(part_keys[0], (POINTS, DIN), 1.0, 6.0, ((0, 8),)),
        "gate_input": noise(part_keys[1], (POINTS, DIN), 1.0, 6.0, ((0, 8),)),
        "state_proj": noise(part_keys[2], (POINTS, 2 * STATE), 1.0, 6.0, ((0, 8),)),
        "step_raw": noise(part_keys[3], (HEADS, POINTS), 1.0, 5.0, ((1, 8),), jnp.float32),
        "decay_log": draw_decay_log(jax.random.fold_in(streams_of[11], 71), part),
        "step_bias": draw_step_bias(jax.random.fold_in(streams_of[11], 71), part),
        "skip_gain": jnp.clip(jax.random.uniform(streams_of[6], (HEADS,), jnp.float32, 0.5, 1.5), 0.5, 1.5),
        "norm_gain": jnp.clip(1.0 + 0.15 * jax.random.normal(streams_of[7], (DIN,), jnp.float32), 0.25, 1.75),
        "out_weight": noise(streams_of[8], (DIN, D), DIN ** -0.5, 0.21875),
        "block_counts": draw_block_counts(jax.random.fold_in(jax.random.fold_in(streams_of[11], part), 71), part),
        "out_cotangent": noise(part_keys[10], (POINTS, D), 1.0, 6.0, ((0, 8),)),
    }


highest = lax.Precision.HIGHEST

def step_decay(step_raw, decay_log, step_bias):
    step_size = jax.nn.softplus(step_raw + step_bias[:, None])
    log_decay = step_size * (-jnp.exp(decay_log))[:, None]
    return (step_size, log_decay)

def group_scan(state_now, pieces):
    x_group, b_group, c_group, step_group, decay_group = pieces
    cumulative = jnp.cumsum(decay_group, axis=1)
    length = cumulative.shape[1]
    lower_mask = (jnp.arange(length)[:, None] >= jnp.arange(length)[None, :])[None]
    spread = jnp.where(lower_mask, cumulative[:, :, None] - cumulative[:, None, :], 0.0)
    weights = jnp.where(lower_mask, jnp.exp(spread), 0.0)
    scores = jnp.dot(c_group, b_group.T, precision=highest)
    mixing = scores[None] * weights * step_group[:, None, :]
    y_local = jnp.einsum('hij,jhp->ihp', mixing, x_group, precision=highest)
    y_carry = jnp.einsum('in,hnp->ihp', c_group, state_now, precision=highest) * jnp.exp(cumulative).T[:, :, None]
    tail_weight = jnp.exp(cumulative[:, -1:] - cumulative) * step_group
    state_next = jnp.exp(cumulative[:, -1])[:, None, None] * state_now + jnp.einsum('hj,jn,jhp->hnp', tail_weight, b_group, x_group, precision=highest)
    return (state_next, y_local + y_carry)

def gated_norm(y_ssd, gate_f, norm_gain):
    mixed = y_ssd * jax.nn.silu(gate_f)
    inverse_rms = lax.rsqrt(lax.optimization_barrier(jnp.mean(mixed * mixed, axis=-1, keepdims=True)) + 1e-05)
    return mixed * inverse_rms * norm_gain

def forward_all(ssm_f, gate_f, proj_f, step_raw, decay_log, step_bias, skip_gain, norm_gain):
    total_rows, row_width = ssm_f.shape
    head_count = decay_log.shape[0]
    head_dim = row_width // head_count
    state_dim = proj_f.shape[1] // 2
    step_size, log_decay = step_decay(step_raw, decay_log, step_bias)
    groups = total_rows // GROUP
    x_all = ssm_f.reshape(groups, GROUP, head_count, head_dim)
    b_all = proj_f[:, :state_dim].reshape(groups, GROUP, state_dim)
    c_all = proj_f[:, state_dim:].reshape(groups, GROUP, state_dim)
    step_all = step_size.reshape(head_count, groups, GROUP).transpose(1, 0, 2)
    decay_all = log_decay.reshape(head_count, groups, GROUP).transpose(1, 0, 2)
    zero_state = jnp.zeros((head_count, state_dim, head_dim), jnp.float32)
    _, y_all = lax.scan(jax.checkpoint(group_scan), zero_state, (x_all, b_all, c_all, step_all, decay_all))
    y_ssd = y_all.reshape(total_rows, row_width) + ssm_f * jnp.repeat(skip_gain, head_dim)[None, :]
    return gated_norm(y_ssd, gate_f, norm_gain)

def regroup_order(block_counts, blocks_dev):
    shards = block_counts.shape[0]
    upper_counts = jnp.concatenate([jnp.diagonal(block_counts, 1), jnp.zeros((1,), jnp.int32)]).astype(jnp.int32)
    lower_counts = jnp.concatenate([jnp.zeros((1,), jnp.int32), jnp.diagonal(block_counts, -1)]).astype(jnp.int32)
    target = jnp.arange(shards * blocks_dev, dtype=jnp.int32)
    shard_of = target // blocks_dev
    within = target % blocks_dev
    before_count = lower_counts[shard_of]
    after_count = upper_counts[shard_of]
    shift = jnp.where(within < before_count, -before_count, jnp.where(within >= blocks_dev - after_count, after_count, 0))
    return (target + shift).astype(jnp.int32)

def regroup(row_data, block_ids):
    blocks = row_data.reshape(block_ids.shape[0], BLOCK_ROWS, -1)
    return blocks[block_ids].reshape(row_data.shape)

def reference(ssm_input, gate_input, state_proj, step_raw, decay_log, step_bias, skip_gain, norm_gain, out_weight, block_counts, out_cotangent):
    ssm_f = ssm_input.astype(jnp.float32)
    gate_f = gate_input.astype(jnp.float32)
    proj_f = state_proj.astype(jnp.float32)
    normed_f, pullback = jax.vjp(forward_all, ssm_f, gate_f, proj_f, step_raw, decay_log, step_bias, skip_gain, norm_gain)
    normed = normed_f.astype(jnp.bfloat16)
    block_ids = regroup_order(block_counts, BLOCKS_DEV)
    out_rows = jnp.dot(normed, out_weight, preferred_element_type=jnp.float32).astype(jnp.bfloat16)
    mixed_points = regroup(out_rows, block_ids)
    returned = regroup(out_cotangent, block_ids)
    g_normed = jnp.dot(returned, out_weight.T, preferred_element_type=jnp.float32)
    grad_scale = POINTS ** (-0.5)
    grad_weight = jnp.dot(normed.T, returned, preferred_element_type=jnp.float32) * grad_scale
    cotangents = pullback(g_normed)
    grad_heads = jnp.stack([cotangents[4], cotangents[5], cotangents[6]]) * grad_scale
    grad_norm = cotangents[7] * grad_scale
    return (mixed_points, cotangents[0].astype(jnp.bfloat16), cotangents[1].astype(jnp.bfloat16), cotangents[2].astype(jnp.bfloat16), cotangents[3], grad_weight, grad_heads, grad_norm)
```

```python
import functools

import jax
import jax.numpy as jnp
from jax import lax
from jax.experimental import pallas as pl
from jax.experimental.pallas import tpu as pltpu
from jax.sharding import PartitionSpec as P

BLOCK_ROWS = 128
F32 = jnp.float32
BF16 = jnp.bfloat16
VMEM = pl.BlockSpec(memory_space=pltpu.VMEM)
SMEM = pl.BlockSpec(memory_space=pltpu.SMEM)


def sds(shape, dtype):
    return jax.ShapeDtypeStruct(shape, dtype)


def run(kernel, outs, args, specs, name, scratch=(), flops=10**8):
    size = sum(a.size * a.dtype.itemsize for a in args)
    size += sum(o.size * o.dtype.itemsize for o in outs)
    return pl.pallas_call(
        kernel,
        out_shape=outs,
        in_specs=specs,
        out_specs=[VMEM] * len(outs),
        scratch_shapes=list(scratch),
        name=name,
        cost_estimate=pl.CostEstimate(flops=flops, bytes_accessed=size, transcendentals=0),
    )(*args)


def dot(a, b, dims=((1,), (0,))):
    return lax.dot_general(a, b, (dims, ((), ())), preferred_element_type=F32)


def split3(v):
    hi = v.astype(BF16)
    rest = v - hi.astype(F32)
    mid = rest.astype(BF16)
    return hi, mid, (rest - mid.astype(F32)).astype(BF16)


def running_sum(v, keep):
    n = v.shape[1]
    k = lax.broadcasted_iota(jnp.int32, (n, n), 0)
    t = lax.broadcasted_iota(jnp.int32, (n, n), 1)
    ones = jnp.where(keep(k, t), 1.0, 0.0).astype(BF16)
    return sum(dot(part, ones) for part in split3(v))


def column(row):
    n = row.shape[1]
    i = lax.broadcasted_iota(jnp.int32, (n, n), 0)
    j = lax.broadcasted_iota(jnp.int32, (n, n), 1)
    return jnp.sum(jnp.where(i == j, jnp.broadcast_to(row, (n, n)), 0.0), axis=1, keepdims=True)


def softplus(v):
    t = jnp.exp(-jnp.abs(v))
    s = t / (2.0 + t)
    q = s * s
    series = jnp.full_like(q, 1.0 / 19.0)
    for odd in (17, 15, 13, 11, 9, 7, 5, 3):
        series = series * q + 1.0 / odd
    return jnp.maximum(v, 0.0) + 2.0 * s * (series * q + 1.0)


def spread_heads(col, width, heads):
    h = lax.broadcasted_iota(jnp.int32, (heads, width), 0)
    c = lax.broadcasted_iota(jnp.int32, (heads, width), 1)
    per = width // heads
    mine = (c >= h * per) & (c < (h + 1) * per)
    return jnp.sum(jnp.where(mine, col, 0.0), axis=0, keepdims=True)


def gather_heads(row, heads):
    width = row.shape[1]
    h = lax.broadcasted_iota(jnp.int32, (heads, width), 0)
    c = lax.broadcasted_iota(jnp.int32, (heads, width), 1)
    per = width // heads
    mine = (c >= h * per) & (c < (h + 1) * per)
    return jnp.sum(jnp.where(mine, row, 0.0), axis=1, keepdims=True)


def put_message(msg_ref, state, row):
    n, width = state.shape
    msg_ref[0:n, :] = state.astype(BF16)
    parts = [p.astype(F32) for p in split3(row)]
    i = lax.broadcasted_iota(jnp.int32, (8, width), 0)
    block = jnp.zeros((8, width), F32)
    for k, part in enumerate(parts):
        block = jnp.where(i == k, part, block)
    msg_ref[n : n + 8, :] = block.astype(BF16)


def message_row(msg):
    block = msg.astype(F32)
    i = lax.broadcasted_iota(jnp.int32, block.shape, 0)
    return jnp.sum(jnp.where(i < 3, block, 0.0), axis=0, keepdims=True)


def local_state_kernel(raw, dlog, bias, x, proj, msg, tot, dt_out, cum_out, bct_out):
    heads, rows = raw.shape
    width = x.shape[1]
    n = proj.shape[1] // 2
    dt = softplus(raw[...] + column(bias[...]))
    decay = dt * (-jnp.exp(column(dlog[...])))
    cum = running_sum(decay, lambda k, t: k <= t)
    dt_out[...] = dt
    cum_out[...] = cum
    last = cum[:, rows - 1 : rows]
    tail = jnp.exp(last - cum) * dt
    bct = proj[...].astype(F32).T
    bct_out[...] = bct.astype(BF16)
    bt = bct[0:n, :]
    lane = lax.broadcasted_iota(jnp.int32, (n, 128), 1)
    for k in range(width // 128):
        left = (bt * tail[2 * k : 2 * k + 1, :]).astype(BF16)
        right = (bt * tail[2 * k + 1 : 2 * k + 2, :]).astype(BF16)
        cols = slice(128 * k, 128 * k + 128)
        tot[0:n, cols] = jnp.where(lane < 64, dot(left, x[:, cols]), dot(right, x[:, cols]))
    factor = spread_heads(jnp.exp(last), width, heads)
    tot[n : n + 8, :] = jnp.broadcast_to(factor, (8, width))
    put_message(msg, tot[0:n, :], factor)


def join_kernel(first, last, flag, got, tot, *refs):
    refs = list(refs)
    pre = None if first else refs.pop(0)
    pre_out = refs.pop(0)
    n = tot.shape[0] - 8
    theirs = got[0:n, :].astype(F32)
    their_f = message_row(got[n : n + 8, :])
    mine = tot[0:n, :]
    my_f = tot[n : n + 1, :]
    after = flag[0] > 0
    old = jnp.zeros_like(mine) if first else pre[0:n, :]
    old_f = jnp.ones_like(my_f) if first else pre[n : n + 1, :]
    pre_out[0:n, :] = old + jnp.where(after, old_f, 0.0) * theirs
    pre_out[n : n + 8, :] = jnp.broadcast_to(old_f * jnp.where(after, their_f, 1.0), (8, mine.shape[1]))
    msg_out, tot_out = refs
    both = jnp.where(after, 1.0, their_f) * mine + jnp.where(after, my_f, 1.0) * theirs
    tot_out[0:n, :] = both
    tot_out[n : n + 8, :] = jnp.broadcast_to(my_f * their_f, (8, mine.shape[1]))
    put_message(msg_out, both, my_f * their_f)


def back_join_kernel(first, flag, got, tot, fwd_got, fwd_tot, *refs):
    refs = list(refs)
    pre = None if first else refs.pop(0)
    pre_out, msg_out, tot_out = refs
    n = tot.shape[0] - 8
    theirs = got[0:n, :].astype(F32)
    their_f = message_row(fwd_got[n : n + 8, :])
    my_f = fwd_tot[n : n + 1, :]
    mine = tot[0:n, :]
    before = flag[0] <= 0
    old = jnp.zeros_like(mine) if first else pre[0:n, :]
    old_f = jnp.ones_like(my_f) if first else pre[n : n + 1, :]
    pre_out[0:n, :] = old + jnp.where(before, old_f, 0.0) * theirs
    pre_out[n : n + 8, :] = jnp.broadcast_to(old_f * jnp.where(before, their_f, 1.0), (8, mine.shape[1]))
    both = jnp.where(before, 1.0, their_f) * mine + jnp.where(before, my_f, 1.0) * theirs
    extra = tot[n : n + 1, :] + message_row(got[n : n + 8, :])
    tot_out[0:n, :] = both
    tot_out[n : n + 8, :] = jnp.broadcast_to(extra, (8, mine.shape[1]))
    put_message(msg_out, both, extra)


def mixing_kernel(x, proj, bct, dt, cum, skip, xt_out, mix_out, y_out):
    rows, width = x.shape
    heads = dt.shape[0]
    n = proj.shape[1] // 2
    per = width // heads
    xt = x[...].astype(F32).T.astype(BF16)
    xt_out[...] = xt
    lane = lax.broadcasted_iota(jnp.int32, proj.shape, 1)
    b_only = jnp.where(lane < n, proj[...].astype(F32), 0.0).astype(BF16)
    c_first = jnp.concatenate([bct[n : 2 * n, :], bct[n : 2 * n, :]], axis=0)
    scores = dot(b_only, c_first)
    j = lax.broadcasted_iota(jnp.int32, (rows, rows), 0)
    i = lax.broadcasted_iota(jnp.int32, (rows, rows), 1)
    scores = jnp.where(j <= i, scores, 0.0)
    start = (cum[...] - jnp.log(dt[...])).T
    skip_col = column(skip[...])
    for h in range(heads):
        span = slice(h * per, (h + 1) * per)
        weight = jnp.exp(jnp.minimum(cum[h : h + 1, :] - start[:, h : h + 1], 80.0))
        mix = (weight * scores).astype(BF16)
        mix_out[h] = mix
        x_h = xt[span, :]
        y_out[span, :] = dot(x_h, mix) + skip_col[h : h + 1, :] * x_h.astype(F32)


def returned_kernel(blocks, pos, counts, cot, got_a, got_b, gate, weight, ret_out, gn_out, zt_out):
    me = pos[0]
    prev = jnp.where(me > 0, counts[me, jnp.maximum(me - 1, 0)], 0)
    nxt = jnp.where(me < blocks - 1, counts[me, jnp.minimum(me + 1, blocks - 1)], 0)
    odd = lax.rem(me, 2) == 1
    rows = cot.shape[0]
    a = got_a[...].astype(F32)
    b = got_b[...].astype(F32)
    own = cot[...].astype(F32)
    ret_out[...] = cot[...]
    from_prev = jnp.where(odd, a, b)
    from_next = jnp.where(odd, b, a)
    ret_out[0:BLOCK_ROWS, :] = jnp.where(prev > 0, from_prev, own[0:BLOCK_ROWS, :]).astype(BF16)
    ret_out[rows - BLOCK_ROWS : rows, :] = jnp.where(
        nxt > 0, from_next, own[rows - BLOCK_ROWS : rows, :]
    ).astype(BF16)
    gn_out[...] = dot(weight[...], ret_out[...], ((1,), (1,)))
    zt_out[...] = gate[...].astype(F32).T.astype(BF16)


def norm_kernel(
    flag, got, pre, y_part, zt, gn, gain, bct, cum,
    sin_out, normed_out, g_out, gz_out, msg, tot, row_out,
    carry, y_all, ge, gnn,
):
    width, rows = y_part.shape
    heads = cum.shape[0]
    n = bct.shape[0] // 2
    per = width // heads
    eps = 1e-05
    state = pre[0:n, :] + jnp.where(flag[0] > 0, pre[n : n + 1, :], 0.0) * got[0:n, :].astype(F32)
    sin_out[...] = state
    carry[...] = dot(state.T.astype(BF16), bct[n : 2 * n, :])
    grow = jnp.exp(cum[...])
    gain_col = jnp.broadcast_to(gain[...], (8, width)).T[:, 0:1]
    squares = jnp.zeros((per, rows), F32)
    cross = jnp.zeros((per, rows), F32)
    for h in range(heads):
        span = slice(h * per, (h + 1) * per)
        y = y_part[span, :] + carry[span, :] * grow[h : h + 1, :]
        y_all[span, :] = y
        z = zt[span, :].astype(F32)
        u = y * (z / (1.0 + jnp.exp(-z)))
        squares += u * u
        cross += u * (gn[span, :] * gain_col[span, :])
    mean = jnp.sum(squares, axis=0, keepdims=True) / width
    inv = lax.rsqrt(mean + eps)
    pull = jnp.sum(cross, axis=0, keepdims=True) / width * inv * inv * inv
    for h in range(heads):
        span = slice(h * per, (h + 1) * per)
        y = y_all[span, :]
        z = zt[span, :].astype(F32)
        sig = 1.0 / (1.0 + jnp.exp(-z))
        s = z * sig
        u = y * s
        scaled = u * inv
        g_n = gn[span, :]
        normed_out[span, :] = (scaled * gain_col[span, :]).astype(BF16)
        gnn[span, :] = (g_n * scaled).astype(BF16)
        g_u = inv * (g_n * gain_col[span, :]) - u * pull
        gz_out[span, :] = (g_u * y * (sig + s * (1.0 - sig))).astype(BF16)
        g_b = (g_u * s).astype(BF16)
        g_out[span, :] = g_b
        g_f = g_b.astype(F32)
        row_out[h : h + 1, :] = jnp.sum(g_f * y, axis=0, keepdims=True)
        ge[span, :] = (g_f * grow[h : h + 1, :]).astype(BF16)
    back = dot(bct[n : 2 * n, :], ge[...], ((1,), (1,)))
    ones = jnp.ones((8, rows), BF16)
    g_gain = dot(ones, gnn[...], ((1,), (1,)))[0:1, :]
    tot[0:n, :] = back
    tot[n : n + 8, :] = jnp.broadcast_to(g_gain, (8, width))
    put_message(msg, back, g_gain)


def weight_kernel(flip, bit, normed, ret, out):
    half = out.shape[0]
    which = (1 - bit[0]) if flip else bit[0]
    part = normed[pl.ds(pl.multiple_of(which * half, half), half), :]
    out[...] = dot(part, ret[...]).astype(out.dtype)


def rows_kernel(normed, weight, out):
    out[...] = dot(normed[...].astype(F32).T.astype(BF16), weight[...]).astype(BF16)


def pick_kernel(blocks, pos, counts, own, got_a, got_b, out):
    me = pos[0]
    prev = jnp.where(me > 0, counts[me, jnp.maximum(me - 1, 0)], 0)
    nxt = jnp.where(me < blocks - 1, counts[me, jnp.minimum(me + 1, blocks - 1)], 0)
    odd = lax.rem(me, 2) == 1
    rows = own.shape[0]
    a = got_a[...].astype(F32)
    b = got_b[...].astype(F32)
    mine = own[...].astype(F32)
    out[...] = own[...]
    out[0:BLOCK_ROWS, :] = jnp.where(
        prev > 0, jnp.where(odd, a, b), mine[0:BLOCK_ROWS, :]
    ).astype(BF16)
    out[rows - BLOCK_ROWS : rows, :] = jnp.where(
        nxt > 0, jnp.where(odd, b, a), mine[rows - BLOCK_ROWS : rows, :]
    ).astype(BF16)


def back_mix_kernel(
    x, xt, g, mix, proj, bct, dt, cum, sin, gz,
    v_out, dbc_out, col_out, xg_out, gate_out, ds, ge,
):
    width, rows = xt.shape
    heads = dt.shape[0]
    n = bct.shape[0] // 2
    per = width // heads
    start = (cum[...] - jnp.log(dt[...])).T
    grow = jnp.exp(cum[...])
    lane = lax.broadcasted_iota(jnp.int32, (rows, 128), 1)
    for h in range(heads):
        span = slice(h * per, (h + 1) * per)
        k = h // 2
        v = dot(g[span, :], mix[h], ((1,), (1,)))
        v_out[span, :] = v
        x_f = xt[span, :].astype(F32)
        g_f = g[span, :].astype(F32)
        col_out[h : h + 1, :] = jnp.sum(x_f * v, axis=0, keepdims=True)
        xg_out[h : h + 1, :] = jnp.sum(x_f * g_f, axis=0, keepdims=True)
        ge[span, :] = (g_f * grow[h : h + 1, :]).astype(BF16)
        mine = (lane >= 64) if h % 2 else (lane < 64)
        x_pair = jnp.where(mine, x[:, 128 * k : 128 * k + 128].astype(F32), 0.0).astype(BF16)
        pair = dot(x_pair, g[128 * k : 128 * k + 128, :])
        weight = jnp.exp(jnp.minimum(cum[h : h + 1, :] - start[:, h : h + 1], 80.0))
        if h == 0:
            ds[...] = weight * pair
        else:
            ds[...] += weight * pair
    j = lax.broadcasted_iota(jnp.int32, (rows, rows), 0)
    i = lax.broadcasted_iota(jnp.int32, (rows, rows), 1)
    d_score = jnp.where(j <= i, ds[...], 0.0).astype(BF16)
    dbc_out[0:n, :] = dot(bct[n : 2 * n, :], d_score, ((1,), (1,)))
    dbc_out[n : 2 * n, :] = dot(bct[0:n, :], d_score) + dot(sin[...].astype(BF16), ge[...])
    gate_out[...] = gz[...].astype(F32).T.astype(BF16)


def final_kernel(
    flag, got, pre, tot, raw, dlog, bias, skip, dt, cum, xt, g, v, bct, dbc, col, row, xg, sin,
    dx_out, dproj_out, step_out, heads_out, gain_out, xs, dxt, later,
):
    width, rows = xt.shape
    heads = dt.shape[0]
    n = bct.shape[0] // 2
    per = width // heads
    grad = pre[0:n, :] + jnp.where(flag[0] <= 0, pre[n : n + 1, :], 0.0) * got[0:n, :].astype(F32)
    gain_out[...] = jnp.broadcast_to(
        tot[n : n + 1, :] + message_row(got[n : n + 8, :]), gain_out.shape
    )
    dt_v = dt[...]
    cum_v = cum[...]
    last = cum_v[:, rows - 1 : rows]
    tail = jnp.exp(last - cum_v)
    tail_dt = tail * dt_v
    skip_col = column(skip[...])
    grad_b = grad.astype(BF16)
    bg = dot(grad.T.astype(BF16), bct[0:n, :])
    for h in range(heads):
        span = slice(h * per, (h + 1) * per)
        x_f = xt[span, :].astype(F32)
        part = bg[span, :] * tail_dt[h : h + 1, :]
        dxt[span, :] = skip_col[h : h + 1, :] * g[span, :].astype(F32) + v[span, :] + part
        later[h : h + 1, :] = jnp.sum(x_f * part, axis=0, keepdims=True)
        xs[span, :] = (x_f * tail_dt[h : h + 1, :]).astype(BF16)
    d_b = dbc[0:n, :] + dot(grad_b, xs[...])
    dproj_out[...] = jnp.concatenate([d_b, dbc[n : 2 * n, :]], axis=0).T.astype(BF16)
    dx_out[...] = dxt[...].T.astype(BF16)
    later_v = later[...]
    inner = row[...] - skip_col * xg[...] - col[...]
    through = gather_heads(jnp.sum(grad * sin[...], axis=0, keepdims=True), heads) * jnp.exp(last)
    d_decay = running_sum(inner, lambda k, t: k >= t) + running_sum(later_v, lambda k, t: k < t) + through
    rate = -jnp.exp(column(dlog[...]))
    d_dt = d_decay * rate + (col[...] + later_v) / dt_v
    lifted = raw[...] + column(bias[...])
    d_raw = d_dt / (1.0 + jnp.exp(-lifted))
    step_out[...] = d_raw
    total = lambda t: jnp.sum(t, axis=1, keepdims=True)
    lane = lax.broadcasted_iota(jnp.int32, heads_out.shape, 1)
    heads_out[...] = jnp.where(
        lane == 0, total(d_decay * dt_v * rate), jnp.where(lane == 1, total(d_raw), total(xg[...]))
    )


def body(
    ssm_input, gate_input, state_proj, step_raw, decay_log, step_bias, skip_gain, norm_gain,
    out_weight, block_counts, out_cotangent,
):
    rows, width = ssm_input.shape
    heads = decay_log.shape[0]
    n = state_proj.shape[1] // 2
    model = out_weight.shape[1]
    shards = lax.axis_size("seq")
    grad_scale = float(rows * shards) ** (-0.5)
    levels = shards.bit_length() - 1
    assert shards == 1 << levels and levels >= 1
    me = lax.axis_index("seq").astype(jnp.int32)
    pos = me.reshape(1)
    bits = [((me >> k) & 1).reshape(1) for k in range(levels)]
    swaps = [[(i, i ^ (1 << k)) for i in range(shards)] for k in range(levels)]
    odd_pairs = [(i, i + 1) for i in range(1, shards - 1, 2)]
    odd_pairs = odd_pairs + [(j, i) for i, j in odd_pairs]

    def trade(value, k):
        return lax.ppermute(value, "seq", swaps[k])

    dlog, bias, skip, gain = (v.reshape(1, -1) for v in (decay_log, step_bias, skip_gain, norm_gain))

    def edges(value):
        first, last = value[:BLOCK_ROWS], value[rows - BLOCK_ROWS :]
        even = (me & 1) == 0
        return (
            trade(jnp.where(even, last, first), 0),
            lax.ppermute(jnp.where(even, first, last), "seq", odd_pairs),
        )

    msg, tot, dt, cum, bct = run(
        local_state_kernel,
        [sds((n + 8, width), BF16), sds((n + 8, width), F32), sds((heads, rows), F32),
         sds((heads, rows), F32), sds((2 * n, rows), BF16)],
        (step_raw, dlog, bias, ssm_input, state_proj), [VMEM] * 5, "local_state",
    )
    fwd_got, fwd_tot, pre = [], [tot], None
    got = trade(msg, 0)
    cot_a, cot_b = edges(out_cotangent)
    xt, mix, y_part = run(
        mixing_kernel,
        [sds((width, rows), BF16), sds((heads, rows, rows), BF16), sds((width, rows), F32)],
        (ssm_input, state_proj, bct, dt, cum, skip), [VMEM] * 6, "mixing",
    )
    ret, gn, zt = run(
        functools.partial(returned_kernel, shards),
        [sds((rows, model), BF16), sds((width, rows), F32), sds((width, rows), BF16)],
        (pos, block_counts, out_cotangent, cot_a, cot_b, gate_input, out_weight),
        [SMEM, SMEM] + [VMEM] * 5, "returned",
    )
    for k in range(levels - 1):
        fwd_got.append(got)
        args = (bits[k], got, tot) + (() if k == 0 else (pre,))
        pre, msg, tot = run(
            functools.partial(join_kernel, k == 0, False),
            [sds((n + 8, width), F32), sds((n + 8, width), BF16), sds((n + 8, width), F32)],
            args, [SMEM] + [VMEM] * (len(args) - 1), f"join{k}",
        )
        fwd_tot.append(tot)
        got = trade(msg, k + 1)
    if pre is None:
        pre = jnp.concatenate([jnp.zeros((n, width), F32), jnp.ones((8, width), F32)])
    fwd_got.append(got)
    sin, normed, g, gz, msg, tot, row = run(
        norm_kernel,
        [sds((n, width), F32), sds((width, rows), BF16), sds((width, rows), BF16),
         sds((width, rows), BF16), sds((n + 8, width), BF16), sds((n + 8, width), F32),
         sds((heads, rows), F32)],
        (bits[levels - 1], got, pre, y_part, zt, gn, gain, bct, cum), [SMEM] + [VMEM] * 8, "norm",
        [pltpu.VMEM((width, rows), F32), pltpu.VMEM((width, rows), F32),
         pltpu.VMEM((width, rows), BF16), pltpu.VMEM((width, rows), BF16)],
    )
    got = trade(msg, 0)

    half = width // 2
    send, keep = (
        run(
            functools.partial(weight_kernel, flip), [sds((half, model), BF16 if flip else F32)],
            (bits[0], normed, ret), [SMEM, VMEM, VMEM], f"weight{int(flip)}",
        )[0]
        for flip in (True, False)
    )
    part = keep + trade(send, 0).astype(F32)
    for k in range(1, levels):
        two = part.reshape(2, part.shape[0] // 2, model)
        bit = bits[k][0]
        send = lax.dynamic_index_in_dim(two, 1 - bit, 0, keepdims=False).astype(BF16)
        part = lax.dynamic_index_in_dim(two, bit, 0, keepdims=False) + trade(send, k).astype(F32)

    (out_rows,) = run(
        rows_kernel, [sds((rows, model), BF16)], (normed, out_weight), [VMEM] * 2, "rows"
    )
    v, dbc, col, xg, grad_gate = run(
        back_mix_kernel,
        [sds((width, rows), F32), sds((2 * n, rows), F32), sds((heads, rows), F32),
         sds((heads, rows), F32), sds((rows, width), BF16)],
        (ssm_input, xt, g, mix, state_proj, bct, dt, cum, sin, gz), [VMEM] * 10, "back_mix",
        [pltpu.VMEM((rows, rows), F32), pltpu.VMEM((width, rows), BF16)],
    )
    row_a, row_b = edges(out_rows)
    (mixed,) = run(
        functools.partial(pick_kernel, shards), [sds((rows, model), BF16)],
        (pos, block_counts, out_rows, row_a, row_b), [SMEM, SMEM] + [VMEM] * 3, "pick",
    )
    pre = None
    for k in range(levels - 1):
        args = (bits[k], got, tot, fwd_got[k], fwd_tot[k]) + (() if k == 0 else (pre,))
        pre, msg, tot = run(
            functools.partial(back_join_kernel, k == 0),
            [sds((n + 8, width), F32), sds((n + 8, width), BF16), sds((n + 8, width), F32)],
            args, [SMEM] + [VMEM] * (len(args) - 1), f"back_join{k}",
        )
        got = trade(msg, k + 1)
    if pre is None:
        pre = jnp.concatenate([jnp.zeros((n, width), F32), jnp.ones((8, width), F32)])
    grad_input, grad_proj, grad_step, head_part, gain_total = run(
        final_kernel,
        [sds((rows, width), BF16), sds((rows, 2 * n), BF16), sds((heads, rows), F32),
         sds((heads, 128), F32), sds((8, width), F32)],
        (bits[levels - 1], got, pre, tot, step_raw, dlog, bias, skip, dt, cum, xt, g, v, bct, dbc,
         col, row, xg, sin), [SMEM] + [VMEM] * 18, "final",
        [pltpu.VMEM((width, rows), BF16), pltpu.VMEM((width, rows), F32),
         pltpu.VMEM((heads, rows), F32)],
    )

    piece = part.astype(BF16)
    sums = head_part
    for k in reversed(range(levels)):
        other = trade(piece, k)
        sums = sums + trade(sums, k)
        bit = bits[k][0]
        piece = jnp.concatenate(
            [jnp.where(bit == 0, piece, other), jnp.where(bit == 0, other, piece)], axis=0
        )
    grad_weight = piece.astype(F32) * grad_scale
    grad_heads = sums[:, :3].T * grad_scale
    grad_norm = gain_total[0] * grad_scale
    return (mixed, grad_input, grad_gate, grad_proj, grad_step, grad_weight, grad_heads, grad_norm)


def solution(mesh):
    return jax.shard_map(
        body,
        mesh=mesh,
        in_specs=(
            P(("geo", "seq"), None),
            P(("geo", "seq"), None),
            P(("geo", "seq"), None),
            P(None, ("geo", "seq")),
            P(),
            P(),
            P(),
            P(),
            P(),
            P("geo", None),
            P(("geo", "seq"), None),
        ),
        out_specs=(
            P(("geo", "seq"), None),
            P(("geo", "seq"), None),
            P(("geo", "seq"), None),
            P(("geo", "seq"), None),
            P(None, ("geo", "seq")),
            P("geo", None),
            P("geo", None),
            P("geo"),
        ),
        check_vma=False,
    )
```
